32 devices in a mesh: dp: 16 (over z, x, core), tensor: 2 (over y).
Axes of the slice: x: 2, y: 2, z: 4, core: 2. Of those that a mesh axis runs over, the one named last changes fastest.
Arguments:
- tokens: bfloat16 [16384, 1024], P(('dp', 'tensor')), may hold values from -6 to 6
- cotangent: bfloat16 [16384, 1024], P(('dp', 'tensor')), may hold values from -6 to 6
- lengths: int32 [16, 4], P('dp'), may hold values from 1 to 512, 1024 in all within a row
- w_in: bfloat16 [1024, 3, 1024], P('dp', None, 'tensor'), may hold values from -0.1875 to 0.1875
- w_out: bfloat16 [1024, 1024], P('tensor', 'dp'), may hold values from -0.1875 to 0.1875
- w_gate_up: bfloat16 [1024, 2, 4608], P('dp', None, 'tensor'), may hold values from -0.1875 to 0.1875
- w_down: bfloat16 [4608, 1024], P('tensor', 'dp'), may hold values from -0.1875 to 0.1875
- conv_weight: float32 [3, 1024], P(None, 'tensor'), may hold values from -3 to 3
- norm_gains: float32 [2, 1024], replicated, may hold values from 0.1 to 1.9
Outputs:
- block_out: bfloat16 [16384, 1024], P(('dp', 'tensor'))
- grad_tokens: bfloat16 [16384, 1024], P(('dp', 'tensor'))
- grad_w_in: float32 [1024, 3, 1024], P('dp', None, 'tensor')
- grad_w_out: float32 [1024, 1024], P('tensor', 'dp')
- grad_w_gate_up: float32 [1024, 2, 4608], P('dp', None, 'tensor')
- grad_w_down: float32 [4608, 1024], P('tensor', 'dp')
- grad_conv_weight: float32 [3, 1024], P(None, 'tensor')
- grad_norm_gains: float32 [2, 1024], replicated
The draws below stay inside these ranges and needn't reach their ends.
Inputs may be any that keep to these rules, and one draw needn't show every extreme that they name: Each row of lengths sums to 1024, and its largest entry is exactly 512.
All inputs are finite; a program needn't handle non-finite values.
Results may differ from the reference program's by a relative error of at most 0.015.
Values may be sent and summed in bfloat16 or wider, within the bound.
A program may use at most 192 MiB of HBM per device.

```python
import math
import jax
import jax.numpy as jnp
import numpy as np
from jax import lax

D = 1024
FF = 4608
TAPS = 3
MAXLEN = 512
ROWS_DP = 1024
SEQS = 4
TOKENS = 16384
N_DP = 16


def levels(rng, extent, cuts, least, top_value):
    factor_of = 1.0
    for dim, blocks in cuts:
        draws = jax.random.uniform(jax.random.fold_in(jax.random.fold_in(rng, 6), dim), (blocks,), jnp.float32, least / len(cuts), top_value / len(cuts))
        factor_of = factor_of * jnp.repeat(jnp.exp(draws), extent[dim] // blocks).reshape((-1,) + (1,) * (len(extent) - 1 - dim))
    return factor_of


def length_profile(amount, total, bound, skew):
    weights = [(1 << 20) // math.isqrt(rank ** skew) + 1 for rank in range(2, amount + 1)]
    surplus, holding = total - bound - (amount - 1), [1] * (amount - 1)
    while surplus > 0:
        movable = [i for i in range(amount - 1) if holding[i] < bound]
        whole, budget = sum([weights[i] for i in movable]), surplus
        for i in movable:
            addition = min(bound - holding[i], max(1, budget * weights[i] // whole), surplus)
            holding[i] = holding[i] + addition
            surplus = surplus - addition
    return np.array([bound] + holding)


def uneven(own_key, number_of, total, reach, lean):
    if number_of == 2:
        one = jax.random.randint(own_key, (), max(1, total - reach), min(reach, total - 1) + 1)
        return jnp.stack([one, total - one])
    sizes = jnp.asarray(length_profile(number_of, total, reach, lean), jnp.int32)
    couples = (number_of - 1) // 2
    giver, receiver = sizes[1:1 + 2 * couples:2], sizes[2:2 + 2 * couples:2]
    slack = jnp.minimum(giver - 1, reach - receiver)
    moved = jax.random.randint(jax.random.fold_in(own_key, 1), (couples,), 0, 1 << 20) % (slack + 1)
    sizes = sizes.at[1:1 + 2 * couples:2].set(giver - moved).at[2:2 + 2 * couples:2].set(receiver + moved)
    return sizes[jax.random.permutation(jax.random.fold_in(own_key, 2), number_of)]


def scatter_about(own_key, dims, deviation, limit, shards=(), kind=jnp.bfloat16):
    result = deviation * jax.random.normal(own_key, dims, jnp.float32)
    if shards:
        result = result * levels(own_key, dims, shards, -0.22, 0.18)
    return jnp.clip(result, -limit, limit).astype(kind)


def setup_inputs(seed: int = 0) -> dict:
    key_of = jax.random.split(jax.random.key(seed), 10)
    return {
        "tokens": scatter_about(key_of[0], (TOKENS, D), 1.0, 6.0, ((0, 32),)),
        "cotangent": scatter_about(key_of[1], (TOKENS, D), 1.0, 6.0, ((0, 32),)),
        "lengths": jax.vmap(lambda own: uneven(own, SEQS, ROWS_DP, MAXLEN, 2))(jax.random.split(key_of[2], N_DP)).reshape((N_DP, SEQS)).astype(jnp.int32),
        "w_in": scatter_about(key_of[3], (D, 3, D), D ** -0.5, 0.1875, ((0, 16), (2, 2))),
        "w_out": scatter_about(key_of[4], (D, D), D ** -0.5, 0.1875, ((0, 2), (1, 16))),
        "w_gate_up": scatter_about(key_of[5], (D, 2, FF), D ** -0.5, 0.1875, ((0, 16), (2, 2))),
        "w_down": scatter_about(key_of[6], (FF, D), (FF // 4) ** -0.5, 0.1875, ((0, 2), (1, 16))),
        "conv_weight": scatter_about(key_of[7], (TAPS, D), 0.6, 3.0, ((1, 2),), jnp.float32),
        "norm_gains": jnp.clip(1.0 + 0.18 * jax.random.normal(key_of[8], (2, D), jnp.float32), 0.1, 1.9),
    }


epsilon = 1e-05

def positions(seq_lengths, row_count):
    seq_lengths = seq_lengths.astype(jnp.int32)
    starts = (jnp.cumsum(seq_lengths) - seq_lengths).astype(jnp.int32)
    row_index = jnp.arange(row_count, dtype=jnp.int32)
    begun_at = jnp.where(starts[None, :] <= row_index[:, None], starts[None, :], jnp.int32(0))
    return (row_index - lax.optimization_barrier(jnp.max(begun_at, axis=1))).astype(jnp.int32)

def delayed(values, steps):
    return jnp.concatenate([jnp.zeros((steps, values.shape[1]), values.dtype), values[:-steps]], 0)

def advanced(values, steps):
    return jnp.concatenate([values[steps:], jnp.zeros((steps, values.shape[1]), values.dtype)], 0)

def one_group(x_rows, cot_rows, seq_lengths, w_in, w_out, w_gate_up, w_down, conv_weight, norm_gains):
    row_count = x_rows.shape[0]
    position = positions(seq_lengths, row_count)
    first_keep = (position >= 1).astype(jnp.float32)[:, None]
    second_keep = (position >= 2).astype(jnp.float32)[:, None]
    x_float = x_rows.astype(jnp.float32)
    rms_first = lax.rsqrt(lax.optimization_barrier(jnp.mean(x_float * x_float, axis=1, keepdims=True)) + epsilon)
    normed_first = (x_float * rms_first * norm_gains[0]).astype(jnp.bfloat16)
    flat_in = w_in.reshape(D, 3 * D)
    projected = jnp.dot(normed_first, flat_in, preferred_element_type=jnp.float32)
    proj_b = projected[:, :D]
    proj_c = projected[:, D:2 * D]
    proj_x = projected[:, 2 * D:]
    gated_in = proj_b * proj_x
    conv_out = conv_weight[0] * gated_in + conv_weight[1] * delayed(gated_in, 1) * first_keep + conv_weight[2] * delayed(gated_in, 2) * second_keep
    mixer_in = (proj_c * conv_out).astype(jnp.bfloat16)
    residual_mid = x_float + jnp.dot(mixer_in, w_out, preferred_element_type=jnp.float32)
    rms_second = lax.rsqrt(lax.optimization_barrier(jnp.mean(residual_mid * residual_mid, axis=1, keepdims=True)) + epsilon)
    normed_second = (residual_mid * rms_second * norm_gains[1]).astype(jnp.bfloat16)
    flat_gu = w_gate_up.reshape(D, 2 * FF)
    gate_up = jnp.dot(normed_second, flat_gu, preferred_element_type=jnp.float32)
    gate_pre = gate_up[:, :FF]
    up_pre = gate_up[:, FF:]
    sig_gate = jax.nn.sigmoid(gate_pre)
    hidden_act = (gate_pre * sig_gate * up_pre).astype(jnp.bfloat16)
    block_out = (residual_mid + jnp.dot(hidden_act, w_down, preferred_element_type=jnp.float32)).astype(jnp.bfloat16)
    grad_act = jnp.dot(cot_rows, w_down.T, preferred_element_type=jnp.float32)
    grad_down = jnp.dot(hidden_act.T, cot_rows, preferred_element_type=jnp.float32)
    grad_gate = (grad_act * up_pre * sig_gate * (1.0 + gate_pre * (1.0 - sig_gate))).astype(jnp.bfloat16)
    grad_up = (grad_act * gate_pre * sig_gate).astype(jnp.bfloat16)
    grad_hidden = jnp.concatenate([grad_gate, grad_up], 1)
    grad_gu = jnp.dot(normed_second.T, grad_hidden, preferred_element_type=jnp.float32).reshape(D, 2, FF)
    grad_normed2 = jnp.dot(grad_hidden, flat_gu.T, preferred_element_type=jnp.float32)
    scaled_two = grad_normed2 * norm_gains[1]
    grad_mid = cot_rows.astype(jnp.float32) + rms_second * scaled_two - residual_mid * (rms_second * rms_second * rms_second) * lax.optimization_barrier(jnp.mean(scaled_two * residual_mid, axis=1, keepdims=True))
    gain_two = lax.optimization_barrier(jnp.sum(grad_normed2 * residual_mid * rms_second, axis=0))
    grad_mid_b = grad_mid.astype(jnp.bfloat16)
    grad_mixer_in = jnp.dot(grad_mid_b, w_out.T, preferred_element_type=jnp.float32)
    grad_wout = jnp.dot(mixer_in.T, grad_mid_b, preferred_element_type=jnp.float32)
    grad_conv_out = grad_mixer_in * proj_c
    grad_gated = conv_weight[0] * grad_conv_out + conv_weight[1] * advanced(grad_conv_out * first_keep, 1) + conv_weight[2] * advanced(grad_conv_out * second_keep, 2)
    grad_taps = jnp.stack([lax.optimization_barrier(jnp.sum(grad_conv_out * gated_in, axis=0)), lax.optimization_barrier(jnp.sum(grad_conv_out * first_keep * delayed(gated_in, 1), axis=0)), lax.optimization_barrier(jnp.sum(grad_conv_out * second_keep * delayed(gated_in, 2), axis=0))])
    grad_proj = jnp.concatenate([grad_gated * proj_x, grad_mixer_in * conv_out, grad_gated * proj_b], 1).astype(jnp.bfloat16)
    grad_win = jnp.dot(normed_first.T, grad_proj, preferred_element_type=jnp.float32).reshape(D, 3, D)
    grad_normed1 = jnp.dot(grad_proj, flat_in.T, preferred_element_type=jnp.float32)
    scaled_one = grad_normed1 * norm_gains[0]
    grad_tokens = (grad_mid + rms_first * scaled_one - x_float * (rms_first * rms_first * rms_first) * lax.optimization_barrier(jnp.mean(scaled_one * x_float, axis=1, keepdims=True))).astype(jnp.bfloat16)
    gain_one = lax.optimization_barrier(jnp.sum(grad_normed1 * x_float * rms_first, axis=0))
    grads = (grad_win, grad_wout, grad_gu, grad_down, grad_taps, jnp.stack([gain_one, gain_two]))
    return (block_out, grad_tokens, grads)

def reference(tokens, cotangent, lengths, w_in, w_out, w_gate_up, w_down, conv_weight, norm_gains):
    x_groups = tokens.reshape(N_DP, ROWS_DP, D)
    cot_groups = cotangent.reshape(N_DP, ROWS_DP, D)
    initial = (jnp.zeros((D, 3, D), jnp.float32), jnp.zeros((D, D), jnp.float32), jnp.zeros((D, 2, FF), jnp.float32), jnp.zeros((FF, D), jnp.float32), jnp.zeros((TAPS, D), jnp.float32), jnp.zeros((2, D), jnp.float32))

    def step_group(totals, inputs):
        x_rows, cot_rows, seq_lengths = inputs
        block_out, grad_tokens, grads = one_group(x_rows, cot_rows, seq_lengths, w_in, w_out, w_gate_up, w_down, conv_weight, norm_gains)
        totals = tuple((total + grad for total, grad in zip(totals, grads)))
        return (totals, (block_out, grad_tokens))
    totals, stacked = lax.scan(step_group, initial, (x_groups, cot_groups, lengths))
    block_out = stacked[0].reshape(TOKENS, D)
    grad_tokens = stacked[1].reshape(TOKENS, D)
    return (block_out, grad_tokens, totals[0], totals[1], totals[2], totals[3], totals[4], totals[5])
```

```python
import jax
import jax.numpy as jnp
from jax import lax
from jax.sharding import PartitionSpec as P

epsilon = 1e-05


def positions(seq_lengths, row_count):
    starts = jnp.cumsum(seq_lengths) - seq_lengths
    row_index = jnp.arange(row_count, dtype=jnp.int32)
    begun_at = jnp.where(starts[None, :] <= row_index[:, None], starts[None, :], jnp.int32(0))
    return row_index - jnp.max(begun_at, axis=1)


def delayed(values, steps):
    return jnp.concatenate([jnp.zeros((steps, values.shape[1]), values.dtype), values[:-steps]], 0)


def advanced(values, steps):
    return jnp.concatenate([values[steps:], jnp.zeros((steps, values.shape[1]), values.dtype)], 0)


def gather_rows(values):
    count = lax.axis_size("tensor")
    if count != 2:
        return lax.all_gather(values, "tensor", axis=0, tiled=True)
    rows = values.shape[0]
    index = lax.axis_index("tensor")
    other = lax.ppermute(values, "tensor", [(0, 1), (1, 0)])
    whole = jnp.zeros((2 * rows, values.shape[1]), values.dtype)
    whole = lax.dynamic_update_slice_in_dim(whole, values, index * rows, 0)
    return lax.dynamic_update_slice_in_dim(whole, other, (1 - index) * rows, 0)


def scatter_rows(values):
    count = lax.axis_size("tensor")
    if count != 2:
        return lax.psum_scatter(
            values.astype(jnp.bfloat16), "tensor", scatter_dimension=0, tiled=True
        ).astype(jnp.float32)
    rows = values.shape[0] // 2
    index = lax.axis_index("tensor")
    away = lax.dynamic_slice_in_dim(values, (1 - index) * rows, rows, 0).astype(jnp.bfloat16)
    other = lax.ppermute(away, "tensor", [(0, 1), (1, 0)])
    return lax.dynamic_slice_in_dim(values, index * rows, rows, 0) + other.astype(jnp.float32)


def butterfly_sum(values, axis):
    count = lax.axis_size(axis)
    if count & (count - 1):
        return lax.psum(values, axis)
    step = 1
    while step < count:
        values = values + lax.ppermute(values, axis, [(i, i ^ step) for i in range(count)])
        step *= 2
    return values


def body(tokens, cotangent, lengths, w_in, w_out, w_gate_up, w_down, conv_weight, norm_gains):
    shard_rows, taken, chan_count = w_in.shape
    hidden = w_gate_up.shape[2]
    packed = jnp.concatenate([w_in.reshape(shard_rows, taken * chan_count), w_out.T], axis=1)
    full_mix = lax.all_gather(packed, "dp", axis=0, tiled=True)
    full_gu = lax.all_gather(
        w_gate_up.reshape(shard_rows, 2 * hidden), "dp", axis=0, tiled=True
    )
    full_down = lax.all_gather(w_down.T, "dp", axis=0, tiled=True)
    full_in = full_mix[:, : taken * chan_count]
    full_out = full_mix[:, taken * chan_count :]
    x_float = tokens.astype(jnp.float32)
    rms_first = lax.rsqrt(jnp.mean(x_float * x_float, axis=1, keepdims=True) + epsilon)
    normed_first = (x_float * rms_first * norm_gains[0]).astype(jnp.bfloat16)
    first_all = gather_rows(normed_first)
    cot_all = gather_rows(cotangent)
    row_count = first_all.shape[0]
    position = positions(lengths[0], row_count)
    first_keep = (position >= 1).astype(jnp.float32)[:, None]
    second_keep = (position >= 2).astype(jnp.float32)[:, None]
    projected = jnp.dot(first_all, full_in, preferred_element_type=jnp.float32)
    proj_b = projected[:, :chan_count]
    proj_c = projected[:, chan_count : 2 * chan_count]
    proj_x = projected[:, 2 * chan_count :]
    gated_in = proj_b * proj_x
    conv_out = (
        conv_weight[0] * gated_in
        + conv_weight[1] * delayed(gated_in, 1) * first_keep
        + conv_weight[2] * delayed(gated_in, 2) * second_keep
    )
    mixer_in = (proj_c * conv_out).astype(jnp.bfloat16)
    residual_mid = x_float + scatter_rows(
        jnp.einsum("rc,dc->rd", mixer_in, full_out, preferred_element_type=jnp.float32)
    )
    rms_second = lax.rsqrt(jnp.mean(residual_mid * residual_mid, axis=1, keepdims=True) + epsilon)
    normed_second = (residual_mid * rms_second * norm_gains[1]).astype(jnp.bfloat16)
    second_all = gather_rows(normed_second)
    gate_up = jnp.dot(second_all, full_gu, preferred_element_type=jnp.float32)
    gate_pre = gate_up[:, :hidden]
    up_pre = gate_up[:, hidden:]
    sig_gate = jax.nn.sigmoid(gate_pre)
    hidden_act = (gate_pre * sig_gate * up_pre).astype(jnp.bfloat16)
    grad_down = jnp.einsum("rd,rf->df", cot_all, hidden_act, preferred_element_type=jnp.float32)
    sum_down = lax.psum_scatter(
        grad_down.astype(jnp.bfloat16), "dp", scatter_dimension=0, tiled=True
    )
    grad_act = jnp.einsum("rd,df->rf", cot_all, full_down, preferred_element_type=jnp.float32)
    grad_gate = (grad_act * up_pre * sig_gate * (1.0 + gate_pre * (1.0 - sig_gate))).astype(
        jnp.bfloat16
    )
    grad_up = (grad_act * gate_pre * sig_gate).astype(jnp.bfloat16)
    grad_hidden = jnp.concatenate([grad_gate, grad_up], axis=1)
    grad_gu = jnp.einsum("rd,rf->df", second_all, grad_hidden, preferred_element_type=jnp.float32)
    sum_gu = lax.psum_scatter(
        grad_gu.astype(jnp.bfloat16), "dp", scatter_dimension=0, tiled=True
    )
    grad_normed2 = scatter_rows(
        jnp.einsum("rf,df->rd", grad_hidden, full_gu, preferred_element_type=jnp.float32)
    )
    block_out = (
        residual_mid
        + scatter_rows(
            jnp.einsum("rf,df->rd", hidden_act, full_down, preferred_element_type=jnp.float32)
        )
    ).astype(jnp.bfloat16)
    scaled_two = grad_normed2 * norm_gains[1]
    grad_mid = (
        cotangent.astype(jnp.float32)
        + rms_second * scaled_two
        - residual_mid
        * (rms_second * rms_second * rms_second)
        * jnp.mean(scaled_two * residual_mid, axis=1, keepdims=True)
    )
    gain_two = jnp.sum(grad_normed2 * residual_mid * rms_second, axis=0)
    mid_all = gather_rows(grad_mid.astype(jnp.bfloat16))
    grad_mixer_in = jnp.dot(mid_all, full_out, preferred_element_type=jnp.float32)
    grad_wout = jnp.einsum("rd,rc->dc", mid_all, mixer_in, preferred_element_type=jnp.float32)
    grad_conv_out = grad_mixer_in * proj_c
    grad_gated = (
        conv_weight[0] * grad_conv_out
        + conv_weight[1] * advanced(grad_conv_out * first_keep, 1)
        + conv_weight[2] * advanced(grad_conv_out * second_keep, 2)
    )
    grad_taps = jnp.stack(
        [
            jnp.sum(grad_conv_out * gated_in, axis=0),
            jnp.sum(grad_conv_out * first_keep * delayed(gated_in, 1), axis=0),
            jnp.sum(grad_conv_out * second_keep * delayed(gated_in, 2), axis=0),
        ]
    )
    grad_proj = jnp.concatenate(
        [grad_gated * proj_x, grad_mixer_in * conv_out, grad_gated * proj_b], axis=1
    ).astype(jnp.bfloat16)
    grad_win = jnp.einsum("rd,rf->df", first_all, grad_proj, preferred_element_type=jnp.float32)
    sum_mix = lax.psum_scatter(
        jnp.concatenate([grad_win.astype(jnp.bfloat16), grad_wout.astype(jnp.bfloat16)], axis=1),
        "dp",
        scatter_dimension=0,
        tiled=True,
    )
    grad_normed1 = scatter_rows(
        jnp.einsum("rf,df->rd", grad_proj, full_in, preferred_element_type=jnp.float32)
    )
    scaled_one = grad_normed1 * norm_gains[0]
    grad_tokens = (
        grad_mid
        + rms_first * scaled_one
        - x_float
        * (rms_first * rms_first * rms_first)
        * jnp.mean(scaled_one * x_float, axis=1, keepdims=True)
    ).astype(jnp.bfloat16)
    gain_one = jnp.sum(grad_normed1 * x_float * rms_first, axis=0)
    model_width = tokens.shape[1]
    sums = butterfly_sum(
        jnp.concatenate([gain_one, gain_two, grad_taps.reshape(-1)]).reshape(-1, 128), "dp"
    ).reshape(-1)
    gain_sums = butterfly_sum(sums[: 2 * model_width].reshape(2, model_width), "tensor")
    grad_conv = sums[2 * model_width :].reshape(grad_taps.shape)
    split = taken * chan_count
    shard_in = sum_mix[:, :split].astype(jnp.float32).reshape(w_in.shape)
    shard_out = sum_mix[:, split:].astype(jnp.float32).T
    shard_gu = sum_gu.astype(jnp.float32).reshape(w_gate_up.shape)
    shard_down = sum_down.astype(jnp.float32).T
    return (block_out, grad_tokens, shard_in, shard_out, shard_gu, shard_down, grad_conv, gain_sums)


def solution(mesh):
    return jax.shard_map(
        body,
        mesh=mesh,
        in_specs=(
            P(("dp", "tensor"), None),
            P(("dp", "tensor"), None),
            P("dp", None),
            P("dp", None, "tensor"),
            P("tensor", "dp"),
            P("dp", None, "tensor"),
            P("tensor", "dp"),
            P(None, "tensor"),
            P(),
        ),
        out_specs=(
            P(("dp", "tensor"), None),
            P(("dp", "tensor"), None),
            P("dp", None, "tensor"),
            P("tensor", "dp"),
            P("dp", None, "tensor"),
            P("tensor", "dp"),
            P(None, "tensor"),
            P(),
        ),
        check_vma=False,
    )
```

```python
import jax
import jax.numpy as jnp
from jax import lax
from jax.sharding import PartitionSpec as P

epsilon = 1e-05


def positions(seq_lengths, row_count):
    starts = jnp.cumsum(seq_lengths) - seq_lengths
    row_index = jnp.arange(row_count, dtype=jnp.int32)
    begun_at = jnp.where(starts[None, :] <= row_index[:, None], starts[None, :], jnp.int32(0))
    return row_index - jnp.max(begun_at, axis=1)


def delayed(values, steps):
    return jnp.concatenate([jnp.zeros((steps, values.shape[1]), values.dtype), values[:-steps]], 0)


def advanced(values, steps):
    return jnp.concatenate([values[steps:], jnp.zeros((steps, values.shape[1]), values.dtype)], 0)


def gather_rows(values):
    count = lax.axis_size("tensor")
    if count != 2:
        return lax.all_gather(values, "tensor", axis=0, tiled=True)
    rows = values.shape[0]
    index = lax.axis_index("tensor")
    other = lax.ppermute(values, "tensor", [(0, 1), (1, 0)])
    whole = jnp.zeros((2 * rows, values.shape[1]), values.dtype)
    whole = lax.dynamic_update_slice_in_dim(whole, values, index * rows, 0)
    return lax.dynamic_update_slice_in_dim(whole, other, (1 - index) * rows, 0)


def scatter_rows(values):
    count = lax.axis_size("tensor")
    if count != 2:
        return lax.psum_scatter(
            values.astype(jnp.bfloat16), "tensor", scatter_dimension=0, tiled=True
        ).astype(jnp.float32)
    rows = values.shape[0] // 2
    index = lax.axis_index("tensor")
    away = lax.dynamic_slice_in_dim(values, (1 - index) * rows, rows, 0).astype(jnp.bfloat16)
    other = lax.ppermute(away, "tensor", [(0, 1), (1, 0)])
    return lax.dynamic_slice_in_dim(values, index * rows, rows, 0) + other.astype(jnp.float32)


def butterfly_sum(values, axis):
    count = lax.axis_size(axis)
    if count & (count - 1):
        return lax.psum(values, axis)
    step = 1
    while step < count:
        values = values + lax.ppermute(values, axis, [(i, i ^ step) for i in range(count)])
        step *= 2
    return values


def gather_blocks(shard, axis):
    count = lax.axis_size(axis)
    if count & (count - 1):
        return lax.all_gather(shard, axis, axis=0, tiled=True)
    index = lax.axis_index(axis)
    blocks = shard[None]
    step = count // 2
    while step >= 1:
        other = lax.ppermute(blocks, axis, [(i, i ^ step) for i in range(count)])
        upper = (index // step) % 2 == 1
        first = jnp.where(upper, other, blocks)
        second = jnp.where(upper, blocks, other)
        blocks = jnp.stack([first, second], axis=1).reshape((-1,) + shard.shape)
        step //= 2
    return blocks.reshape((-1,) + shard.shape[1:])


def scatter_blocks(values, axis):
    count = lax.axis_size(axis)
    if count & (count - 1):
        return lax.psum_scatter(values, axis, scatter_dimension=0, tiled=True)
    index = lax.axis_index(axis)
    shape = (values.shape[0] // count,) + values.shape[1:]
    step = 1
    while step < count:
        pairs = values.reshape((count // step // 2, 2) + shape)
        side = (index // step) % 2
        away = lax.dynamic_index_in_dim(pairs, 1 - side, 1, keepdims=False)
        kept = lax.dynamic_index_in_dim(pairs, side, 1, keepdims=False)
        other = lax.ppermute(away, axis, [(i, i ^ step) for i in range(count)])
        values = (kept.astype(jnp.float32) + other.astype(jnp.float32)).astype(values.dtype)
        step *= 2
    return values.reshape(shape)


def body(tokens, cotangent, lengths, w_in, w_out, w_gate_up, w_down, conv_weight, norm_gains):
    shard_rows, taken, chan_count = w_in.shape
    hidden = w_gate_up.shape[2]
    packed = jnp.concatenate([w_in.reshape(shard_rows, taken * chan_count), w_out.T], axis=1)
    full_mix = lax.all_gather(packed, "dp", axis=0, tiled=True)
    full_gu = lax.all_gather(
        w_gate_up.reshape(shard_rows, 2 * hidden), "dp", axis=0, tiled=True
    )
    full_down = gather_blocks(w_down.T, "dp")
    full_in = full_mix[:, : taken * chan_count]
    full_out = full_mix[:, taken * chan_count :]
    x_float = tokens.astype(jnp.float32)
    rms_first = lax.rsqrt(jnp.mean(x_float * x_float, axis=1, keepdims=True) + epsilon)
    normed_first = (x_float * rms_first * norm_gains[0]).astype(jnp.bfloat16)
    first_all = gather_rows(normed_first)
    cot_all = gather_rows(cotangent)
    row_count = first_all.shape[0]
    position = positions(lengths[0], row_count)
    first_keep = (position >= 1).astype(jnp.float32)[:, None]
    second_keep = (position >= 2).astype(jnp.float32)[:, None]
    projected = jnp.dot(first_all, full_in, preferred_element_type=jnp.float32)
    proj_b = projected[:, :chan_count]
    proj_c = projected[:, chan_count : 2 * chan_count]
    proj_x = projected[:, 2 * chan_count :]
    gated_in = proj_b * proj_x
    conv_out = (
        conv_weight[0] * gated_in
        + conv_weight[1] * delayed(gated_in, 1) * first_keep
        + conv_weight[2] * delayed(gated_in, 2) * second_keep
    )
    mixer_in = (proj_c * conv_out).astype(jnp.bfloat16)
    residual_mid = x_float + scatter_rows(
        jnp.einsum("rc,dc->rd", mixer_in, full_out, preferred_element_type=jnp.float32)
    )
    rms_second = lax.rsqrt(jnp.mean(residual_mid * residual_mid, axis=1, keepdims=True) + epsilon)
    normed_second = (residual_mid * rms_second * norm_gains[1]).astype(jnp.bfloat16)
    second_all = gather_rows(normed_second)
    gate_up = jnp.dot(second_all, full_gu, preferred_element_type=jnp.float32)
    gate_pre = gate_up[:, :hidden]
    up_pre = gate_up[:, hidden:]
    sig_gate = jax.nn.sigmoid(gate_pre)
    hidden_act = (gate_pre * sig_gate * up_pre).astype(jnp.bfloat16)
    grad_down = jnp.einsum("rd,rf->df", cot_all, hidden_act, preferred_element_type=jnp.float32)
    grad_down, full_down = lax.optimization_barrier((grad_down.astype(jnp.bfloat16), full_down))
    sum_down = lax.psum_scatter(grad_down, "dp", scatter_dimension=0, tiled=True)
    grad_act = jnp.einsum("rd,df->rf", cot_all, full_down, preferred_element_type=jnp.float32)
    grad_gate = (grad_act * up_pre * sig_gate * (1.0 + gate_pre * (1.0 - sig_gate))).astype(
        jnp.bfloat16
    )
    grad_up = (grad_act * gate_pre * sig_gate).astype(jnp.bfloat16)
    grad_hidden = jnp.concatenate([grad_gate, grad_up], axis=1)
    grad_gu = jnp.einsum("rd,rf->df", second_all, grad_hidden, preferred_element_type=jnp.float32)
    grad_gu, grad_gate, grad_up = lax.optimization_barrier(
        (grad_gu.astype(jnp.bfloat16), grad_gate, grad_up)
    )
    grad_hidden = jnp.concatenate([grad_gate, grad_up], axis=1)
    grad_gu, sum_down = lax.optimization_barrier((grad_gu, sum_down))
    sum_gu = lax.psum_scatter(grad_gu, "dp", scatter_dimension=0, tiled=True)
    grad_normed2 = scatter_rows(
        jnp.einsum("rf,df->rd", grad_hidden, full_gu, preferred_element_type=jnp.float32)
    )
    block_out = (
        residual_mid
        + scatter_rows(
            jnp.einsum("rf,df->rd", hidden_act, full_down, preferred_element_type=jnp.float32)
        )
    ).astype(jnp.bfloat16)
    scaled_two = grad_normed2 * norm_gains[1]
    grad_mid = (
        cotangent.astype(jnp.float32)
        + rms_second * scaled_two
        - residual_mid
        * (rms_second * rms_second * rms_second)
        * jnp.mean(scaled_two * residual_mid, axis=1, keepdims=True)
    )
    gain_two = jnp.sum(grad_normed2 * residual_mid * rms_second, axis=0)
    mid_all = gather_rows(grad_mid.astype(jnp.bfloat16))
    grad_mixer_in = jnp.dot(mid_all, full_out, preferred_element_type=jnp.float32)
    grad_wout = jnp.einsum("rd,rc->dc", mid_all, mixer_in, preferred_element_type=jnp.float32)
    grad_conv_out = grad_mixer_in * proj_c
    grad_gated = (
        conv_weight[0] * grad_conv_out
        + conv_weight[1] * advanced(grad_conv_out * first_keep, 1)
        + conv_weight[2] * advanced(grad_conv_out * second_keep, 2)
    )
    grad_taps = jnp.stack(
        [
            jnp.sum(grad_conv_out * gated_in, axis=0),
            jnp.sum(grad_conv_out * first_keep * delayed(gated_in, 1), axis=0),
            jnp.sum(grad_conv_out * second_keep * delayed(gated_in, 2), axis=0),
        ]
    )
    grad_proj = jnp.concatenate(
        [grad_gated * proj_x, grad_mixer_in * conv_out, grad_gated * proj_b], axis=1
    ).astype(jnp.bfloat16)
    grad_win = jnp.einsum("rd,rf->df", first_all, grad_proj, preferred_element_type=jnp.float32)
    grad_mix = jnp.concatenate(
        [grad_win.astype(jnp.bfloat16), grad_wout.astype(jnp.bfloat16)], axis=1
    )
    sum_mix = scatter_blocks(grad_mix, "dp")
    grad_normed1 = scatter_rows(
        jnp.einsum("rf,df->rd", grad_proj, full_in, preferred_element_type=jnp.float32)
    )
    scaled_one = grad_normed1 * norm_gains[0]
    grad_tokens = (
        grad_mid
        + rms_first * scaled_one
        - x_float
        * (rms_first * rms_first * rms_first)
        * jnp.mean(scaled_one * x_float, axis=1, keepdims=True)
    ).astype(jnp.bfloat16)
    gain_one = jnp.sum(grad_normed1 * x_float * rms_first, axis=0)
    model_width = tokens.shape[1]
    sums = butterfly_sum(
        jnp.concatenate([gain_one, gain_two, grad_taps.reshape(-1)]).reshape(-1, 128), "dp"
    ).reshape(-1)
    gain_sums = butterfly_sum(sums[: 2 * model_width].reshape(2, model_width), "tensor")
    grad_conv = sums[2 * model_width :].reshape(grad_taps.shape)
    split = taken * chan_count
    shard_in = sum_mix[:, :split].astype(jnp.float32).reshape(w_in.shape)
    shard_out = sum_mix[:, split:].astype(jnp.float32).T
    shard_gu = sum_gu.astype(jnp.float32).reshape(w_gate_up.shape)
    shard_down = sum_down.astype(jnp.float32).T
    return (block_out, grad_tokens, shard_in, shard_out, shard_gu, shard_down, grad_conv, gain_sums)


def solution(mesh):
    return jax.shard_map(
        body,
        mesh=mesh,
        in_specs=(
            P(("dp", "tensor"), None),
            P(("dp", "tensor"), None),
            P("dp", None),
            P("dp", None, "tensor"),
            P("tensor", "dp"),
            P("dp", None, "tensor"),
            P("tensor", "dp"),
            P(None, "tensor"),
            P(),
        ),
        out_specs=(
            P(("dp", "tensor"), None),
            P(("dp", "tensor"), None),
            P("dp", None, "tensor"),
            P("tensor", "dp"),
            P("dp", None, "tensor"),
            P("tensor", "dp"),
            P(None, "tensor"),
            P(),
        ),
        check_vma=False,
    )
```
